32 devices in a mesh: groups: 2 (over y), head: 8 (over z, x), blk: 2 (over core).
Axes of the slice: x: 2, y: 2, z: 4, core: 2. Of those that a mesh axis runs over, the one named last changes fastest.
Arguments:
- queries: bfloat16 [256, 4096], P(('groups', 'head', 'blk')), parts along dimension 0, may hold values from -36 to 36
- keys: bfloat16 [256, 4096], P(('groups', 'head', 'blk')), parts along dimension 0, may hold values from -6 to 6
- values: bfloat16 [256, 4096], P(('groups', 'head', 'blk')), parts along dimension 0, may hold values from -12 to 12
- tile_mask: int32 [64, 1, 1], P('groups'), parts along dimension 0, may hold values from 0 to 1, as said below
Outputs:
- attended: bfloat16 [256, 4096], P(('groups', 'head', 'blk')), parts along dimension 0
The draws below stay inside these ranges and needn't reach their ends.
There are 2 independent parts, one for each index of `groups`. The reference program is written for one: setup_inputs(seed, part) draws one part's arguments, and reference() takes and returns one part's arrays. A program takes and returns all parts, laid end to end along the dimension named above; each array names one. Nothing has to cross between parts.
Inputs may be any that keep to these rules, and one draw needn't show every extreme that they name: tile_mask[h, t, t] = 1 for every head h and query tile t.
All inputs are finite; a program needn't handle non-finite values.
Results may differ from the reference program's by a relative error of at most 0.005.
Values may be sent and summed in bfloat16 or wider, within the bound.
No kernel may reach another device: no remote copies, remote signals or barrier semaphores. Data moves between devices by JAX's collectives and lax.ppermute only.
A program may use at most 64 MiB of HBM per device.

```python
import jax
import jax.numpy as jnp
from jax import lax

H = 32
HD = 128
TILE = 128
QUERIES = 128
KEYS = 128
QTILES = 1
KTILES = 1


def draw_queries(key, part):
    noise_key = jax.random.fold_in(key, 1)
    base = 2.5 * jax.random.truncated_normal(noise_key, -6.0, 6.0, (QUERIES, H, HD), jnp.float32)
    return base.reshape(QUERIES, H * HD).astype(jnp.bfloat16)


def draw_keys(key, part):
    noise_key = jax.random.fold_in(key, 2)
    base = jax.random.truncated_normal(noise_key, -6.0, 6.0, (KEYS, H, HD), jnp.float32)
    return base.reshape(KEYS, H * HD).astype(jnp.bfloat16)


def draw_tile_mask(key, part):
    key = jax.random.fold_in(key, 31)
    key_a, key_b = jax.random.split(key)
    level = jax.random.randint(key_a, (H, 1, 1), 5, 96, dtype=jnp.int32)
    raw = jax.random.randint(key_b, (H, QTILES, KTILES), 0, 100, dtype=jnp.int32)
    diagonal = jnp.arange(QTILES, dtype=jnp.int32) * KTILES // QTILES
    forced = jnp.arange(KTILES, dtype=jnp.int32)[None, :] == diagonal[:, None]
    return jnp.where((raw < level) | forced[None, :, :], 1, 0).astype(jnp.int32)


def block_scale(own_key, shape, cuts, least, largest):
    loudness = 1.0
    for dim, shards_of in cuts:
        draws = jax.random.uniform(jax.random.fold_in(jax.random.fold_in(own_key, 6), dim), (shards_of,), jnp.float32, least / len(cuts), largest / len(cuts))
        loudness = loudness * jnp.repeat(jnp.exp(draws), shape[dim] // shards_of).reshape((-1,) + (1,) * (len(shape) - 1 - dim))
    return loudness


def scatter_about(own_key, shape, width, most, cuts=(), kind=jnp.bfloat16):
    gain = block_scale(own_key, shape, cuts, -0.22, 0.18) if cuts else 1.0
    values = jax.random.normal(own_key, shape, jnp.float32) * width * gain
    return jnp.minimum(jnp.maximum(values, -most), most).astype(kind)


def setup_inputs(seed: int = 0, part: int = 0) -> dict:
    key_list = jax.random.split(jax.random.key(seed), 5)
    part_splits = jax.random.split(jax.random.fold_in(key_list[4], part), 5)
    return {
        "queries": draw_queries(jax.random.fold_in(jax.random.fold_in(key_list[4], part), 71), part),
        "keys": draw_keys(jax.random.fold_in(jax.random.fold_in(key_list[4], part), 71), part),
        "values": scatter_about(part_splits[2], (KEYS, H * HD), 2.0, 12.0, ((0, 16),)),
        "tile_mask": draw_tile_mask(jax.random.fold_in(jax.random.fold_in(key_list[4], part), 71), part),
    }


def reference(queries, keys, values, tile_mask):
    query_count = queries.shape[0]
    key_count = keys.shape[0]
    q_heads = queries.reshape(query_count, H, HD).transpose(1, 0, 2)
    k_heads = keys.reshape(key_count, H, HD).transpose(1, 0, 2)
    v_heads = values.reshape(key_count, H, HD).transpose(1, 0, 2)
    key_tiles = jnp.arange(key_count, dtype=jnp.int32) // TILE
    q_block = 512 if query_count % 512 == 0 else query_count
    score_scale = HD ** -0.5

    def one_head(inputs):
        q_head, k_head, v_head, mask_head = inputs

        def one_block(pieces):
            q_piece, q_tiles = pieces
            scores = jnp.dot(q_piece, k_head.T, preferred_element_type=jnp.float32) * score_scale
            allowed = mask_head[q_tiles][:, key_tiles] > 0
            scores = jnp.where(allowed, scores, -jnp.inf)
            top = jnp.max(scores, axis=1, keepdims=True)
            weights = jnp.where(allowed, jnp.exp(scores - top), 0.0)
            total = jnp.sum(weights, axis=1, keepdims=True)
            summed = jnp.dot(weights.astype(jnp.bfloat16), v_head, preferred_element_type=jnp.float32)
            return (summed / total).astype(jnp.bfloat16)

        tiles_all = (jnp.arange(query_count, dtype=jnp.int32) // TILE).reshape(-1, q_block)
        result = lax.map(one_block, (q_head.reshape(-1, q_block, HD), tiles_all))
        return result.reshape(query_count, HD)

    outputs = lax.map(one_head, (q_heads, k_heads, v_heads, tile_mask))
    return outputs.transpose(1, 0, 2).reshape(query_count, H * HD)
```

```python
import functools

import jax
import jax.numpy as jnp
from jax import lax
from jax.experimental import pallas as pl
from jax.experimental.pallas import tpu as pltpu
from jax.sharding import PartitionSpec as P

H = 32
HD = 128
TILE = 128


big_negative = -1e30


def from_behind(array, axis, by):
    count = lax.axis_size(axis)
    return lax.ppermute(array, axis, [(i, (i + by) % count) for i in range(count)])


def update_block(inputs, k_rows, v_rows, k_tiles, heads_mask, score_scale):
    q_piece, q_tiles, out_sum, row_top, row_total = inputs
    rows_mask = jnp.take(heads_mask, q_tiles, axis=1)
    allowed = jnp.take(rows_mask, k_tiles, axis=2) > 0
    scores = (
        jnp.einsum("qhd,khd->hqk", q_piece, k_rows, preferred_element_type=jnp.float32)
        * score_scale
    )
    scores = jnp.where(allowed, scores, big_negative)
    new_top = jnp.maximum(row_top, jnp.max(scores, axis=2))
    factor = jnp.exp(row_top - new_top)
    weights = jnp.where(allowed, jnp.exp(scores - new_top[:, :, None]), 0.0)
    row_total = row_total * factor + jnp.sum(weights, axis=2)
    out_sum = out_sum * factor[:, :, None] + jnp.einsum(
        "hqk,khd->hqd", weights.astype(jnp.bfloat16), v_rows, preferred_element_type=jnp.float32
    )
    return (out_sum, new_top, row_total)


def attend(q_in, q_index, stacked, key_index_of, pass_on, heads_mask, per_dev, blk_count, my_blk):
    q_rows = q_in.reshape(-1, per_dev, HD)
    row_count = q_rows.shape[0]
    block_count = row_count // row_count
    q_blocks = q_rows.reshape(block_count, row_count, per_dev, HD)
    q_tiles = (q_index // TILE).reshape(block_count, row_count)
    out_sum = jnp.zeros((block_count, per_dev, row_count, HD), jnp.float32)
    row_top = jnp.full((block_count, per_dev, row_count), big_negative, jnp.float32)
    row_total = jnp.zeros((block_count, per_dev, row_count), jnp.float32)
    kv_pair = stacked
    for cycle_step in range(blk_count):
        if cycle_step > 0:
            kv_pair = pass_on(kv_pair)
        k_tiles = key_index_of((my_blk - cycle_step) % blk_count) // TILE
        k_rows = kv_pair[0].reshape(-1, per_dev, HD)
        v_rows = kv_pair[1].reshape(-1, per_dev, HD)

        def step_block(inputs):
            return update_block(inputs, k_rows, v_rows, k_tiles, heads_mask, HD ** (-0.5))

        out_sum, row_top, row_total = lax.map(
            step_block, (q_blocks, q_tiles, out_sum, row_top, row_total)
        )
    out_sum = out_sum.transpose(0, 2, 1, 3).reshape(row_count, per_dev, HD)
    row_top = row_top.transpose(0, 2, 1).reshape(row_count, per_dev)
    row_total = row_total.transpose(0, 2, 1).reshape(row_count, per_dev)
    return (out_sum, row_top, row_total)


def general(queries, keys, values, tile_mask):
    head_count = lax.axis_size("head")
    blk_count = lax.axis_size("blk")
    my_head = lax.axis_index("head")
    my_blk = lax.axis_index("blk")
    per_dev = max(1, H // head_count)
    split_count = max(1, head_count // H)
    groups = head_count // split_count
    row_width = per_dev * HD
    query_count = queries.shape[0]
    key_count = keys.shape[0]
    part_id = my_head % split_count
    heads_mask = lax.dynamic_slice_in_dim(tile_mask, my_head // split_count * per_dev, per_dev, 0)
    source = jnp.arange(head_count, dtype=jnp.int32)

    def copy_rows(matrix, row_count):
        shaped = matrix.reshape(row_count, groups, row_width).transpose(1, 0, 2)[:, None]
        return jnp.broadcast_to(shaped, (groups, split_count, row_count, row_width)).reshape(
            head_count, row_count, row_width
        )

    def index_of(per_source, offset, row_count, src_blk):
        starts = (source[:, None] * blk_count + src_blk) * per_source + offset
        return (starts + jnp.arange(row_count, dtype=jnp.int32)[None, :]).reshape(-1)

    sub_rows = query_count // split_count
    shaped = queries.reshape(split_count, query_count // split_count, groups, row_width)
    q_in = lax.all_to_all(
        shaped.transpose(2, 0, 1, 3).reshape(head_count, query_count // split_count, row_width),
        "head",
        split_axis=0,
        concat_axis=0,
        tiled=True,
    )
    k_in, v_in = (
        lax.all_to_all(copy_rows(keys, key_count), "head", split_axis=0, concat_axis=0, tiled=True),
        lax.all_to_all(
            copy_rows(values, key_count), "head", split_axis=0, concat_axis=0, tiled=True
        ),
    )
    kv_stack = jnp.stack([k_in, v_in])

    def pass_on(kv_pair):
        return from_behind(kv_pair, "blk", 1)

    def key_index_of(src_blk):
        return index_of(key_count, 0, key_count, src_blk)

    q_index = index_of(query_count, part_id * sub_rows, sub_rows, my_blk)
    out_sum, row_top, row_total = attend(
        q_in, q_index, kv_stack, key_index_of, pass_on, heads_mask, per_dev, blk_count, my_blk
    )
    result = (
        (out_sum / row_total[:, :, None])
        .astype(jnp.bfloat16)
        .reshape(head_count, sub_rows, row_width)
    )
    returned = lax.all_to_all(result, "head", split_axis=0, concat_axis=0, tiled=True)
    attended = (
        returned.reshape(groups, split_count, sub_rows, row_width)
        .transpose(1, 2, 0, 3)
        .reshape(query_count, H * HD)
    )
    return attended


def attend_kernel(mask_ref, got_ref, out_ref, *, row_count, per_dev):
    first = (lax.axis_index("head") * lax.axis_size("blk") + lax.axis_index("blk")) * per_dev
    sources = got_ref.shape[0]
    for head in range(per_dev):
        allowed = mask_ref[first + head] > 0
        columns = slice(head * HD, (head + 1) * HD)
        q, k, v = (
            got_ref[:, i * row_count : (i + 1) * row_count, columns].reshape(-1, HD)
            for i in range(3)
        )
        scores = lax.dot_general(
            q, k, (((1,), (1,)), ((), ())), preferred_element_type=jnp.float32
        )
        scores = jnp.where(allowed, scores * HD ** (-0.5), big_negative)
        top = jnp.max(scores, axis=1, keepdims=True)
        weights = jnp.where(allowed, jnp.exp(scores - top), 0.0)
        total = jnp.sum(weights, axis=1, keepdims=True)
        summed = jnp.dot(
            weights.astype(jnp.bfloat16), v, preferred_element_type=jnp.float32
        )
        out_ref[:, :, columns] = (
            (summed / total).astype(jnp.bfloat16).reshape(sources, row_count, HD)
        )


def one_tile(queries, keys, values, tile_mask):
    axes = ("head", "blk")
    count = lax.axis_size(axes)
    row_count = queries.shape[0]
    per_dev = H // count
    width = per_dev * HD
    packed = jnp.concatenate(
        [m.reshape(row_count, count, width).transpose(1, 0, 2) for m in (queries, keys, values)],
        axis=1,
    )
    got = lax.all_to_all(packed, axes, split_axis=0, concat_axis=0, tiled=True)
    result = pl.pallas_call(
        functools.partial(attend_kernel, row_count=row_count, per_dev=per_dev),
        out_shape=jax.ShapeDtypeStruct((count, row_count, width), jnp.bfloat16),
        in_specs=[
            pl.BlockSpec(memory_space=pltpu.SMEM),
            pl.BlockSpec(memory_space=pltpu.VMEM),
        ],
        out_specs=pl.BlockSpec(memory_space=pltpu.VMEM),
        compiler_params=pltpu.CompilerParams(vmem_limit_bytes=4 * 1024 * 1024),
    )(tile_mask.reshape(-1), got)
    returned = lax.all_to_all(result, axes, split_axis=0, concat_axis=0, tiled=True)
    return returned.transpose(1, 0, 2).reshape(row_count, H * HD)


def on_device(queries, keys, values, tile_mask):
    count = lax.axis_size("head") * lax.axis_size("blk")
    same_rows = queries.shape[0] == keys.shape[0]
    if same_rows and queries.shape[0] * count == TILE and H % count == 0:
        return one_tile(queries, keys, values, tile_mask)
    return general(queries, keys, values, tile_mask)


def solution(mesh):
    in_specs = (
        P(("groups", "head", "blk"), None),
        P(("groups", "head", "blk"), None),
        P(("groups", "head", "blk"), None),
        P("groups", None, None),
    )
    out_specs = P(("groups", "head", "blk"), None)
    return jax.shard_map(
        on_device, mesh=mesh, in_specs=in_specs, out_specs=out_specs, check_vma=False
    )
```

```python
import functools

import jax
import jax.numpy as jnp
from jax import lax
from jax.experimental import pallas as pl
from jax.experimental.pallas import tpu as pltpu
from jax.sharding import PartitionSpec as P

H = 32
HD = 128
TILE = 128


big_negative = -1e30


def from_behind(array, axis, by):
    count = lax.axis_size(axis)
    return lax.ppermute(array, axis, [(i, (i + by) % count) for i in range(count)])


def update_block(inputs, k_rows, v_rows, k_tiles, heads_mask, score_scale):
    q_piece, q_tiles, out_sum, row_top, row_total = inputs
    rows_mask = jnp.take(heads_mask, q_tiles, axis=1)
    allowed = jnp.take(rows_mask, k_tiles, axis=2) > 0
    scores = (
        jnp.einsum("qhd,khd->hqk", q_piece, k_rows, preferred_element_type=jnp.float32)
        * score_scale
    )
    scores = jnp.where(allowed, scores, big_negative)
    new_top = jnp.maximum(row_top, jnp.max(scores, axis=2))
    factor = jnp.exp(row_top - new_top)
    weights = jnp.where(allowed, jnp.exp(scores - new_top[:, :, None]), 0.0)
    row_total = row_total * factor + jnp.sum(weights, axis=2)
    out_sum = out_sum * factor[:, :, None] + jnp.einsum(
        "hqk,khd->hqd", weights.astype(jnp.bfloat16), v_rows, preferred_element_type=jnp.float32
    )
    return (out_sum, new_top, row_total)


def attend(q_in, q_index, stacked, key_index_of, pass_on, heads_mask, per_dev, blk_count, my_blk):
    q_rows = q_in.reshape(-1, per_dev, HD)
    row_count = q_rows.shape[0]
    block_count = row_count // row_count
    q_blocks = q_rows.reshape(block_count, row_count, per_dev, HD)
    q_tiles = (q_index // TILE).reshape(block_count, row_count)
    out_sum = jnp.zeros((block_count, per_dev, row_count, HD), jnp.float32)
    row_top = jnp.full((block_count, per_dev, row_count), big_negative, jnp.float32)
    row_total = jnp.zeros((block_count, per_dev, row_count), jnp.float32)
    kv_pair = stacked
    for cycle_step in range(blk_count):
        if cycle_step > 0:
            kv_pair = pass_on(kv_pair)
        k_tiles = key_index_of((my_blk - cycle_step) % blk_count) // TILE
        k_rows = kv_pair[0].reshape(-1, per_dev, HD)
        v_rows = kv_pair[1].reshape(-1, per_dev, HD)

        def step_block(inputs):
            return update_block(inputs, k_rows, v_rows, k_tiles, heads_mask, HD ** (-0.5))

        out_sum, row_top, row_total = lax.map(
            step_block, (q_blocks, q_tiles, out_sum, row_top, row_total)
        )
    out_sum = out_sum.transpose(0, 2, 1, 3).reshape(row_count, per_dev, HD)
    row_top = row_top.transpose(0, 2, 1).reshape(row_count, per_dev)
    row_total = row_total.transpose(0, 2, 1).reshape(row_count, per_dev)
    return (out_sum, row_top, row_total)


def general(queries, keys, values, tile_mask):
    head_count = lax.axis_size("head")
    blk_count = lax.axis_size("blk")
    my_head = lax.axis_index("head")
    my_blk = lax.axis_index("blk")
    per_dev = max(1, H // head_count)
    split_count = max(1, head_count // H)
    groups = head_count // split_count
    row_width = per_dev * HD
    query_count = queries.shape[0]
    key_count = keys.shape[0]
    part_id = my_head % split_count
    heads_mask = lax.dynamic_slice_in_dim(tile_mask, my_head // split_count * per_dev, per_dev, 0)
    source = jnp.arange(head_count, dtype=jnp.int32)

    def copy_rows(matrix, row_count):
        shaped = matrix.reshape(row_count, groups, row_width).transpose(1, 0, 2)[:, None]
        return jnp.broadcast_to(shaped, (groups, split_count, row_count, row_width)).reshape(
            head_count, row_count, row_width
        )

    def index_of(per_source, offset, row_count, src_blk):
        starts = (source[:, None] * blk_count + src_blk) * per_source + offset
        return (starts + jnp.arange(row_count, dtype=jnp.int32)[None, :]).reshape(-1)

    sub_rows = query_count // split_count
    shaped = queries.reshape(split_count, query_count // split_count, groups, row_width)
    q_in = lax.all_to_all(
        shaped.transpose(2, 0, 1, 3).reshape(head_count, query_count // split_count, row_width),
        "head",
        split_axis=0,
        concat_axis=0,
        tiled=True,
    )
    k_in, v_in = (
        lax.all_to_all(copy_rows(keys, key_count), "head", split_axis=0, concat_axis=0, tiled=True),
        lax.all_to_all(
            copy_rows(values, key_count), "head", split_axis=0, concat_axis=0, tiled=True
        ),
    )
    kv_stack = jnp.stack([k_in, v_in])

    def pass_on(kv_pair):
        return from_behind(kv_pair, "blk", 1)

    def key_index_of(src_blk):
        return index_of(key_count, 0, key_count, src_blk)

    q_index = index_of(query_count, part_id * sub_rows, sub_rows, my_blk)
    out_sum, row_top, row_total = attend(
        q_in, q_index, kv_stack, key_index_of, pass_on, heads_mask, per_dev, blk_count, my_blk
    )
    result = (
        (out_sum / row_total[:, :, None])
        .astype(jnp.bfloat16)
        .reshape(head_count, sub_rows, row_width)
    )
    returned = lax.all_to_all(result, "head", split_axis=0, concat_axis=0, tiled=True)
    attended = (
        returned.reshape(groups, split_count, sub_rows, row_width)
        .transpose(1, 2, 0, 3)
        .reshape(query_count, H * HD)
    )
    return attended


def attend_kernel(allowed_ref, got_ref, out_ref, *, per_dev):
    sources, rows, _ = got_ref.shape
    rows = rows // 3
    first = (lax.axis_index("head") * lax.axis_size("blk") + lax.axis_index("blk")) * per_dev
    heads = lax.broadcasted_iota(jnp.int32, allowed_ref.shape, 1)
    for head in range(per_dev):
        allowed = jnp.max(jnp.where(heads == first + head, allowed_ref[...], 0), axis=1, keepdims=True) > 0
        columns = slice(head * HD, (head + 1) * HD)
        q, k, v = (
            got_ref[:, part * rows : (part + 1) * rows, columns].reshape(-1, HD)
            for part in range(3)
        )
        scores = lax.dot_general(
            q, k, (((1,), (1,)), ((), ())), preferred_element_type=jnp.float32
        )
        scores = jnp.where(allowed, scores * HD ** (-0.5), big_negative)
        top = jnp.max(scores, axis=1, keepdims=True)
        weights = jnp.where(allowed, jnp.exp(scores - top), 0.0)
        total = jnp.sum(weights, axis=1, keepdims=True)
        summed = jnp.dot(
            weights.astype(jnp.bfloat16), v, preferred_element_type=jnp.float32
        )
        out_ref[:, :, columns] = (
            (summed / total).astype(jnp.bfloat16).reshape(sources, rows, HD)
        )


def one_tile(queries, keys, values, tile_mask):
    axes = ("head", "blk")
    count = lax.axis_size(axes)
    rows = queries.shape[0]
    per_dev = H // count
    width = per_dev * HD
    vmem = pl.BlockSpec(memory_space=pltpu.VMEM)
    packed = jnp.concatenate(
        [m.reshape(rows, count, width).transpose(1, 0, 2) for m in (queries, keys, values)],
        axis=1,
    )
    packed, tile_mask = lax.optimization_barrier((packed, tile_mask))
    allowed = (tile_mask.reshape(1, H) > 0).astype(jnp.int32)
    packed, allowed = lax.optimization_barrier((packed, allowed))
    got = lax.all_to_all(packed, axes, split_axis=0, concat_axis=0, tiled=True)
    result = pl.pallas_call(
        functools.partial(attend_kernel, per_dev=per_dev),
        out_shape=jax.ShapeDtypeStruct((count, rows, width), jnp.bfloat16),
        in_specs=[vmem] * 2,
        out_specs=vmem,
        compiler_params=pltpu.CompilerParams(vmem_limit_bytes=4 * 1024 * 1024),
    )(allowed, got)
    returned = lax.all_to_all(result, axes, split_axis=0, concat_axis=0, tiled=True)
    return returned.transpose(1, 0, 2).reshape(rows, H * HD)


def on_device(queries, keys, values, tile_mask):
    count = lax.axis_size("head") * lax.axis_size("blk")
    same_rows = queries.shape[0] == keys.shape[0]
    if same_rows and queries.shape[0] * count == TILE and H % count == 0:
        return one_tile(queries, keys, values, tile_mask)
    return general(queries, keys, values, tile_mask)


def solution(mesh):
    in_specs = (
        P(("groups", "head", "blk"), None),
        P(("groups", "head", "blk"), None),
        P(("groups", "head", "blk"), None),
        P("groups", None, None),
    )
    out_specs = P(("groups", "head", "blk"), None)
    return jax.shard_map(
        on_device, mesh=mesh, in_specs=in_specs, out_specs=out_specs, check_vma=False
    )
```

```python
import functools

import jax
import jax.numpy as jnp
from jax import lax
from jax.experimental import pallas as pl
from jax.experimental.pallas import tpu as pltpu
from jax.sharding import PartitionSpec as P

H = 32
HD = 128
TILE = 128


big_negative = -1e30


def from_behind(array, axis, by):
    count = lax.axis_size(axis)
    return lax.ppermute(array, axis, [(i, (i + by) % count) for i in range(count)])


def update_block(inputs, k_rows, v_rows, k_tiles, heads_mask, score_scale):
    q_piece, q_tiles, out_sum, row_top, row_total = inputs
    rows_mask = jnp.take(heads_mask, q_tiles, axis=1)
    allowed = jnp.take(rows_mask, k_tiles, axis=2) > 0
    scores = (
        jnp.einsum("qhd,khd->hqk", q_piece, k_rows, preferred_element_type=jnp.float32)
        * score_scale
    )
    scores = jnp.where(allowed, scores, big_negative)
    new_top = jnp.maximum(row_top, jnp.max(scores, axis=2))
    factor = jnp.exp(row_top - new_top)
    weights = jnp.where(allowed, jnp.exp(scores - new_top[:, :, None]), 0.0)
    row_total = row_total * factor + jnp.sum(weights, axis=2)
    out_sum = out_sum * factor[:, :, None] + jnp.einsum(
        "hqk,khd->hqd", weights.astype(jnp.bfloat16), v_rows, preferred_element_type=jnp.float32
    )
    return (out_sum, new_top, row_total)


def attend(q_in, q_index, stacked, key_index_of, pass_on, heads_mask, per_dev, blk_count, my_blk):
    q_rows = q_in.reshape(-1, per_dev, HD)
    row_count = q_rows.shape[0]
    block_count = row_count // row_count
    q_blocks = q_rows.reshape(block_count, row_count, per_dev, HD)
    q_tiles = (q_index // TILE).reshape(block_count, row_count)
    out_sum = jnp.zeros((block_count, per_dev, row_count, HD), jnp.float32)
    row_top = jnp.full((block_count, per_dev, row_count), big_negative, jnp.float32)
    row_total = jnp.zeros((block_count, per_dev, row_count), jnp.float32)
    kv_pair = stacked
    for cycle_step in range(blk_count):
        if cycle_step > 0:
            kv_pair = pass_on(kv_pair)
        k_tiles = key_index_of((my_blk - cycle_step) % blk_count) // TILE
        k_rows = kv_pair[0].reshape(-1, per_dev, HD)
        v_rows = kv_pair[1].reshape(-1, per_dev, HD)

        def step_block(inputs):
            return update_block(inputs, k_rows, v_rows, k_tiles, heads_mask, HD ** (-0.5))

        out_sum, row_top, row_total = lax.map(
            step_block, (q_blocks, q_tiles, out_sum, row_top, row_total)
        )
    out_sum = out_sum.transpose(0, 2, 1, 3).reshape(row_count, per_dev, HD)
    row_top = row_top.transpose(0, 2, 1).reshape(row_count, per_dev)
    row_total = row_total.transpose(0, 2, 1).reshape(row_count, per_dev)
    return (out_sum, row_top, row_total)


def general(queries, keys, values, tile_mask):
    head_count = lax.axis_size("head")
    blk_count = lax.axis_size("blk")
    my_head = lax.axis_index("head")
    my_blk = lax.axis_index("blk")
    per_dev = max(1, H // head_count)
    split_count = max(1, head_count // H)
    groups = head_count // split_count
    row_width = per_dev * HD
    query_count = queries.shape[0]
    key_count = keys.shape[0]
    part_id = my_head % split_count
    heads_mask = lax.dynamic_slice_in_dim(tile_mask, my_head // split_count * per_dev, per_dev, 0)
    source = jnp.arange(head_count, dtype=jnp.int32)

    def copy_rows(matrix, row_count):
        shaped = matrix.reshape(row_count, groups, row_width).transpose(1, 0, 2)[:, None]
        return jnp.broadcast_to(shaped, (groups, split_count, row_count, row_width)).reshape(
            head_count, row_count, row_width
        )

    def index_of(per_source, offset, row_count, src_blk):
        starts = (source[:, None] * blk_count + src_blk) * per_source + offset
        return (starts + jnp.arange(row_count, dtype=jnp.int32)[None, :]).reshape(-1)

    sub_rows = query_count // split_count
    shaped = queries.reshape(split_count, query_count // split_count, groups, row_width)
    q_in = lax.all_to_all(
        shaped.transpose(2, 0, 1, 3).reshape(head_count, query_count // split_count, row_width),
        "head",
        split_axis=0,
        concat_axis=0,
        tiled=True,
    )
    k_in, v_in = (
        lax.all_to_all(copy_rows(keys, key_count), "head", split_axis=0, concat_axis=0, tiled=True),
        lax.all_to_all(
            copy_rows(values, key_count), "head", split_axis=0, concat_axis=0, tiled=True
        ),
    )
    kv_stack = jnp.stack([k_in, v_in])

    def pass_on(kv_pair):
        return from_behind(kv_pair, "blk", 1)

    def key_index_of(src_blk):
        return index_of(key_count, 0, key_count, src_blk)

    q_index = index_of(query_count, part_id * sub_rows, sub_rows, my_blk)
    out_sum, row_top, row_total = attend(
        q_in, q_index, kv_stack, key_index_of, pass_on, heads_mask, per_dev, blk_count, my_blk
    )
    result = (
        (out_sum / row_total[:, :, None])
        .astype(jnp.bfloat16)
        .reshape(head_count, sub_rows, row_width)
    )
    returned = lax.all_to_all(result, "head", split_axis=0, concat_axis=0, tiled=True)
    attended = (
        returned.reshape(groups, split_count, sub_rows, row_width)
        .transpose(1, 2, 0, 3)
        .reshape(query_count, H * HD)
    )
    return attended


def slot_order(count):
    quarter = count // 4
    return [
        *range(3 * quarter - 1, 2 * quarter - 1, -1),
        *range(count - 1, 3 * quarter - 1, -1),
        *range(2 * quarter - 1, -1, -1),
    ]


def attend_kernel(allowed_ref, got_ref, out_ref, *, per_dev):
    sources, rows, _ = got_ref.shape
    rows = rows // 3
    me = lax.axis_index("head") * lax.axis_size("blk") + lax.axis_index("blk")
    slot = sum(jnp.where(me == d, s, 0) for s, d in enumerate(slot_order(sources)))
    first = slot * per_dev
    heads = lax.broadcasted_iota(jnp.int32, allowed_ref.shape, 1)
    for head in range(per_dev):
        mine = jnp.where(heads == first + head, allowed_ref[...], 0)
        allowed = jnp.max(mine, axis=1, keepdims=True) > 0
        columns = slice(head * HD, (head + 1) * HD)
        q, k, v = (
            got_ref[:, part * rows : (part + 1) * rows, columns].reshape(-1, HD)
            for part in range(3)
        )
        scores = lax.dot_general(
            q, k, (((1,), (1,)), ((), ())), preferred_element_type=jnp.float32
        )
        scores = jnp.where(allowed, scores * HD ** (-0.5), big_negative)
        top = jnp.max(scores, axis=1, keepdims=True)
        weights = jnp.where(allowed, jnp.exp(scores - top), 0.0)
        total = jnp.sum(weights, axis=1, keepdims=True)
        summed = jnp.dot(
            weights.astype(jnp.bfloat16), v, preferred_element_type=jnp.float32
        )
        out_ref[:, :, columns] = (
            (summed / total).astype(jnp.bfloat16).reshape(sources, rows, HD)
        )


def one_tile(queries, keys, values, tile_mask):
    count = lax.axis_size(("head", "blk"))
    rows = queries.shape[0]
    per_dev = H // count
    width = per_dev * HD
    vmem = pl.BlockSpec(memory_space=pltpu.VMEM)
    packed = jnp.concatenate(
        [m.reshape(rows, count, width).transpose(1, 0, 2) for m in (queries, keys, values)],
        axis=1,
    )
    packed, tile_mask = lax.optimization_barrier((packed, tile_mask))
    allowed = (tile_mask.reshape(1, H) > 0).astype(jnp.int32)
    packed, allowed = lax.optimization_barrier((packed, allowed))
    exchange = functools.partial(
        lax.all_to_all,
        axis_name=("head", "blk"),
        split_axis=0,
        concat_axis=0,
        axis_index_groups=[slot_order(count)],
        tiled=True,
    )
    got = exchange(packed)
    result = pl.pallas_call(
        functools.partial(attend_kernel, per_dev=per_dev),
        out_shape=jax.ShapeDtypeStruct((count, rows, width), jnp.bfloat16),
        in_specs=[vmem] * 2,
        out_specs=vmem,
        compiler_params=pltpu.CompilerParams(vmem_limit_bytes=4 * 1024 * 1024),
    )(allowed, got)
    returned = exchange(result)
    return returned.transpose(1, 0, 2).reshape(rows, H * HD)


def on_device(queries, keys, values, tile_mask):
    count = lax.axis_size("head") * lax.axis_size("blk")
    same_rows = queries.shape[0] == keys.shape[0]
    if same_rows and queries.shape[0] * count == TILE and H % count == 0 and count % 4 == 0:
        return one_tile(queries, keys, values, tile_mask)
    return general(queries, keys, values, tile_mask)


def solution(mesh):
    in_specs = (
        P(("groups", "head", "blk"), None),
        P(("groups", "head", "blk"), None),
        P(("groups", "head", "blk"), None),
        P("groups", None, None),
    )
    out_specs = P(("groups", "head", "blk"), None)
    return jax.shard_map(
        on_device, mesh=mesh, in_specs=in_specs, out_specs=out_specs, check_vma=False
    )
```

```python
import functools

import jax
import jax.numpy as jnp
from jax import lax
from jax.experimental import pallas as pl
from jax.experimental.pallas import tpu as pltpu
from jax.sharding import PartitionSpec as P

H = 32
HD = 128
TILE = 128


big_negative = -1e30


def from_behind(array, axis, by):
    count = lax.axis_size(axis)
    return lax.ppermute(array, axis, [(i, (i + by) % count) for i in range(count)])


def update_block(inputs, k_rows, v_rows, k_tiles, heads_mask, score_scale):
    q_piece, q_tiles, out_sum, row_top, row_total = inputs
    rows_mask = jnp.take(heads_mask, q_tiles, axis=1)
    allowed = jnp.take(rows_mask, k_tiles, axis=2) > 0
    scores = (
        jnp.einsum("qhd,khd->hqk", q_piece, k_rows, preferred_element_type=jnp.float32)
        * score_scale
    )
    scores = jnp.where(allowed, scores, big_negative)
    new_top = jnp.maximum(row_top, jnp.max(scores, axis=2))
    factor = jnp.exp(row_top - new_top)
    weights = jnp.where(allowed, jnp.exp(scores - new_top[:, :, None]), 0.0)
    row_total = row_total * factor + jnp.sum(weights, axis=2)
    out_sum = out_sum * factor[:, :, None] + jnp.einsum(
        "hqk,khd->hqd", weights.astype(jnp.bfloat16), v_rows, preferred_element_type=jnp.float32
    )
    return (out_sum, new_top, row_total)


def attend(q_in, q_index, stacked, key_index_of, pass_on, heads_mask, per_dev, blk_count, my_blk):
    q_rows = q_in.reshape(-1, per_dev, HD)
    row_count = q_rows.shape[0]
    block_count = row_count // row_count
    q_blocks = q_rows.reshape(block_count, row_count, per_dev, HD)
    q_tiles = (q_index // TILE).reshape(block_count, row_count)
    out_sum = jnp.zeros((block_count, per_dev, row_count, HD), jnp.float32)
    row_top = jnp.full((block_count, per_dev, row_count), big_negative, jnp.float32)
    row_total = jnp.zeros((block_count, per_dev, row_count), jnp.float32)
    kv_pair = stacked
    for cycle_step in range(blk_count):
        if cycle_step > 0:
            kv_pair = pass_on(kv_pair)
        k_tiles = key_index_of((my_blk - cycle_step) % blk_count) // TILE
        k_rows = kv_pair[0].reshape(-1, per_dev, HD)
        v_rows = kv_pair[1].reshape(-1, per_dev, HD)

        def step_block(inputs):
            return update_block(inputs, k_rows, v_rows, k_tiles, heads_mask, HD ** (-0.5))

        out_sum, row_top, row_total = lax.map(
            step_block, (q_blocks, q_tiles, out_sum, row_top, row_total)
        )
    out_sum = out_sum.transpose(0, 2, 1, 3).reshape(row_count, per_dev, HD)
    row_top = row_top.transpose(0, 2, 1).reshape(row_count, per_dev)
    row_total = row_total.transpose(0, 2, 1).reshape(row_count, per_dev)
    return (out_sum, row_top, row_total)


def general(queries, keys, values, tile_mask):
    head_count = lax.axis_size("head")
    blk_count = lax.axis_size("blk")
    my_head = lax.axis_index("head")
    my_blk = lax.axis_index("blk")
    per_dev = max(1, H // head_count)
    split_count = max(1, head_count // H)
    groups = head_count // split_count
    row_width = per_dev * HD
    query_count = queries.shape[0]
    key_count = keys.shape[0]
    part_id = my_head % split_count
    heads_mask = lax.dynamic_slice_in_dim(tile_mask, my_head // split_count * per_dev, per_dev, 0)
    source = jnp.arange(head_count, dtype=jnp.int32)

    def copy_rows(matrix, row_count):
        shaped = matrix.reshape(row_count, groups, row_width).transpose(1, 0, 2)[:, None]
        return jnp.broadcast_to(shaped, (groups, split_count, row_count, row_width)).reshape(
            head_count, row_count, row_width
        )

    def index_of(per_source, offset, row_count, src_blk):
        starts = (source[:, None] * blk_count + src_blk) * per_source + offset
        return (starts + jnp.arange(row_count, dtype=jnp.int32)[None, :]).reshape(-1)

    sub_rows = query_count // split_count
    shaped = queries.reshape(split_count, query_count // split_count, groups, row_width)
    q_in = lax.all_to_all(
        shaped.transpose(2, 0, 1, 3).reshape(head_count, query_count // split_count, row_width),
        "head",
        split_axis=0,
        concat_axis=0,
        tiled=True,
    )
    k_in, v_in = (
        lax.all_to_all(copy_rows(keys, key_count), "head", split_axis=0, concat_axis=0, tiled=True),
        lax.all_to_all(
            copy_rows(values, key_count), "head", split_axis=0, concat_axis=0, tiled=True
        ),
    )
    kv_stack = jnp.stack([k_in, v_in])

    def pass_on(kv_pair):
        return from_behind(kv_pair, "blk", 1)

    def key_index_of(src_blk):
        return index_of(key_count, 0, key_count, src_blk)

    q_index = index_of(query_count, part_id * sub_rows, sub_rows, my_blk)
    out_sum, row_top, row_total = attend(
        q_in, q_index, kv_stack, key_index_of, pass_on, heads_mask, per_dev, blk_count, my_blk
    )
    result = (
        (out_sum / row_total[:, :, None])
        .astype(jnp.bfloat16)
        .reshape(head_count, sub_rows, row_width)
    )
    returned = lax.all_to_all(result, "head", split_axis=0, concat_axis=0, tiled=True)
    attended = (
        returned.reshape(groups, split_count, sub_rows, row_width)
        .transpose(1, 2, 0, 3)
        .reshape(query_count, H * HD)
    )
    return attended


def slot_order(count):
    quarter = count // 4
    return [
        *range(3 * quarter - 1, 2 * quarter - 1, -1),
        *range(count - 1, 3 * quarter - 1, -1),
        *range(2 * quarter - 1, -1, -1),
    ]


def attend_kernel(allowed_ref, got_ref, out_ref, *, per_dev):
    sources, rows, _ = got_ref.shape
    rows = rows // 3
    me = lax.axis_index("head") * lax.axis_size("blk") + lax.axis_index("blk")
    slot = sum(jnp.where(me == d, s, 0) for s, d in enumerate(slot_order(sources)))
    first = slot * per_dev
    heads = lax.broadcasted_iota(jnp.int32, allowed_ref.shape, 1)
    def part_of(part, head):
        columns = slice(head * HD, (head + 1) * HD)
        return got_ref[:, part * rows : (part + 1) * rows, columns].reshape(-1, HD)

    scores = [
        lax.dot_general(
            part_of(0, head), part_of(1, head), (((1,), (1,)), ((), ())),
            preferred_element_type=jnp.float32,
        )
        for head in range(per_dev)
    ]
    allowed = [
        jnp.max(jnp.where(heads == first + head, allowed_ref[...], 0), axis=1, keepdims=True) > 0
        for head in range(per_dev)
    ]
    weights = []
    for head in range(per_dev):
        masked = jnp.where(allowed[head], scores[head], big_negative)
        top = jnp.max(masked, axis=1, keepdims=True)
        weights.append(jnp.where(allowed[head], jnp.exp((masked - top) * HD ** (-0.5)), 0.0))
    for head in range(per_dev):
        summed = jnp.dot(
            weights[head].astype(jnp.bfloat16), part_of(2, head), preferred_element_type=jnp.float32
        )
        total = jnp.sum(weights[head], axis=1, keepdims=True)
        out_ref[:, :, head * HD : (head + 1) * HD] = (
            (summed * (1.0 / total)).astype(jnp.bfloat16).reshape(sources, rows, HD)
        )


def one_tile(queries, keys, values, tile_mask):
    count = lax.axis_size(("head", "blk"))
    rows = queries.shape[0]
    per_dev = H // count
    width = per_dev * HD
    vmem = pl.BlockSpec(memory_space=pltpu.VMEM)
    packed = jnp.concatenate(
        [m.reshape(rows, count, width).transpose(1, 0, 2) for m in (queries, keys, values)],
        axis=1,
    )
    packed, tile_mask = lax.optimization_barrier((packed, tile_mask))
    allowed = (tile_mask.reshape(1, H) > 0).astype(jnp.int32)
    packed, allowed = lax.optimization_barrier((packed, allowed))
    exchange = functools.partial(
        lax.all_to_all,
        axis_name=("head", "blk"),
        split_axis=0,
        concat_axis=0,
        axis_index_groups=[slot_order(count)],
        tiled=True,
    )
    got = exchange(packed)
    result = pl.pallas_call(
        functools.partial(attend_kernel, per_dev=per_dev),
        out_shape=jax.ShapeDtypeStruct((count, rows, width), jnp.bfloat16),
        in_specs=[vmem] * 2,
        out_specs=vmem,
        compiler_params=pltpu.CompilerParams(vmem_limit_bytes=4 * 1024 * 1024),
    )(allowed, got)
    returned = exchange(result)
    return returned.transpose(1, 0, 2).reshape(rows, H * HD)


def on_device(queries, keys, values, tile_mask):
    count = lax.axis_size("head") * lax.axis_size("blk")
    same_rows = queries.shape[0] == keys.shape[0]
    if same_rows and queries.shape[0] * count == TILE and H % count == 0 and count % 4 == 0:
        return one_tile(queries, keys, values, tile_mask)
    return general(queries, keys, values, tile_mask)


def solution(mesh):
    in_specs = (
        P(("groups", "head", "blk"), None),
        P(("groups", "head", "blk"), None),
        P(("groups", "head", "blk"), None),
        P("groups", None, None),
    )
    out_specs = P(("groups", "head", "blk"), None)
    return jax.shard_map(
        on_device, mesh=mesh, in_specs=in_specs, out_specs=out_specs, check_vma=False
    )
```

```python
import functools

import jax
import jax.numpy as jnp
from jax import lax
from jax.experimental import pallas as pl
from jax.experimental.pallas import tpu as pltpu
from jax.sharding import PartitionSpec as P

H = 32
HD = 128
TILE = 128


big_negative = -1e30


def from_behind(array, axis, by):
    count = lax.axis_size(axis)
    return lax.ppermute(array, axis, [(i, (i + by) % count) for i in range(count)])


def update_block(inputs, k_rows, v_rows, k_tiles, heads_mask, score_scale):
    q_piece, q_tiles, out_sum, row_top, row_total = inputs
    rows_mask = jnp.take(heads_mask, q_tiles, axis=1)
    allowed = jnp.take(rows_mask, k_tiles, axis=2) > 0
    scores = (
        jnp.einsum("qhd,khd->hqk", q_piece, k_rows, preferred_element_type=jnp.float32)
        * score_scale
    )
    scores = jnp.where(allowed, scores, big_negative)
    new_top = jnp.maximum(row_top, jnp.max(scores, axis=2))
    factor = jnp.exp(row_top - new_top)
    weights = jnp.where(allowed, jnp.exp(scores - new_top[:, :, None]), 0.0)
    row_total = row_total * factor + jnp.sum(weights, axis=2)
    out_sum = out_sum * factor[:, :, None] + jnp.einsum(
        "hqk,khd->hqd", weights.astype(jnp.bfloat16), v_rows, preferred_element_type=jnp.float32
    )
    return (out_sum, new_top, row_total)


def attend(q_in, q_index, stacked, key_index_of, pass_on, heads_mask, per_dev, blk_count, my_blk):
    q_rows = q_in.reshape(-1, per_dev, HD)
    row_count = q_rows.shape[0]
    block_count = row_count // row_count
    q_blocks = q_rows.reshape(block_count, row_count, per_dev, HD)
    q_tiles = (q_index // TILE).reshape(block_count, row_count)
    out_sum = jnp.zeros((block_count, per_dev, row_count, HD), jnp.float32)
    row_top = jnp.full((block_count, per_dev, row_count), big_negative, jnp.float32)
    row_total = jnp.zeros((block_count, per_dev, row_count), jnp.float32)
    kv_pair = stacked
    for cycle_step in range(blk_count):
        if cycle_step > 0:
            kv_pair = pass_on(kv_pair)
        k_tiles = key_index_of((my_blk - cycle_step) % blk_count) // TILE
        k_rows = kv_pair[0].reshape(-1, per_dev, HD)
        v_rows = kv_pair[1].reshape(-1, per_dev, HD)

        def step_block(inputs):
            return update_block(inputs, k_rows, v_rows, k_tiles, heads_mask, HD ** (-0.5))

        out_sum, row_top, row_total = lax.map(
            step_block, (q_blocks, q_tiles, out_sum, row_top, row_total)
        )
    out_sum = out_sum.transpose(0, 2, 1, 3).reshape(row_count, per_dev, HD)
    row_top = row_top.transpose(0, 2, 1).reshape(row_count, per_dev)
    row_total = row_total.transpose(0, 2, 1).reshape(row_count, per_dev)
    return (out_sum, row_top, row_total)


def general(queries, keys, values, tile_mask):
    head_count = lax.axis_size("head")
    blk_count = lax.axis_size("blk")
    my_head = lax.axis_index("head")
    my_blk = lax.axis_index("blk")
    per_dev = max(1, H // head_count)
    split_count = max(1, head_count // H)
    groups = head_count // split_count
    row_width = per_dev * HD
    query_count = queries.shape[0]
    key_count = keys.shape[0]
    part_id = my_head % split_count
    heads_mask = lax.dynamic_slice_in_dim(tile_mask, my_head // split_count * per_dev, per_dev, 0)
    source = jnp.arange(head_count, dtype=jnp.int32)

    def copy_rows(matrix, row_count):
        shaped = matrix.reshape(row_count, groups, row_width).transpose(1, 0, 2)[:, None]
        return jnp.broadcast_to(shaped, (groups, split_count, row_count, row_width)).reshape(
            head_count, row_count, row_width
        )

    def index_of(per_source, offset, row_count, src_blk):
        starts = (source[:, None] * blk_count + src_blk) * per_source + offset
        return (starts + jnp.arange(row_count, dtype=jnp.int32)[None, :]).reshape(-1)

    sub_rows = query_count // split_count
    shaped = queries.reshape(split_count, query_count // split_count, groups, row_width)
    q_in = lax.all_to_all(
        shaped.transpose(2, 0, 1, 3).reshape(head_count, query_count // split_count, row_width),
        "head",
        split_axis=0,
        concat_axis=0,
        tiled=True,
    )
    k_in, v_in = (
        lax.all_to_all(copy_rows(keys, key_count), "head", split_axis=0, concat_axis=0, tiled=True),
        lax.all_to_all(
            copy_rows(values, key_count), "head", split_axis=0, concat_axis=0, tiled=True
        ),
    )
    kv_stack = jnp.stack([k_in, v_in])

    def pass_on(kv_pair):
        return from_behind(kv_pair, "blk", 1)

    def key_index_of(src_blk):
        return index_of(key_count, 0, key_count, src_blk)

    q_index = index_of(query_count, part_id * sub_rows, sub_rows, my_blk)
    out_sum, row_top, row_total = attend(
        q_in, q_index, kv_stack, key_index_of, pass_on, heads_mask, per_dev, blk_count, my_blk
    )
    result = (
        (out_sum / row_total[:, :, None])
        .astype(jnp.bfloat16)
        .reshape(head_count, sub_rows, row_width)
    )
    returned = lax.all_to_all(result, "head", split_axis=0, concat_axis=0, tiled=True)
    attended = (
        returned.reshape(groups, split_count, sub_rows, row_width)
        .transpose(1, 2, 0, 3)
        .reshape(query_count, H * HD)
    )
    return attended


def slot_order():
    chips, cores = lax.axis_size("head"), lax.axis_size("blk")
    half = chips // 2
    order = [*range(half + 1, chips), half, half - 1, *range(half - 1)]
    return [chip * cores + core for chip in order for core in reversed(range(cores))]


def attend_kernel(allowed_ref, got_ref, out_ref, *, per_dev):
    sources, rows, _ = got_ref.shape
    rows = rows // 3
    me = lax.axis_index("head") * lax.axis_size("blk") + lax.axis_index("blk")
    slot = sum(jnp.where(me == d, s, 0) for s, d in enumerate(slot_order()))
    first = slot * per_dev
    heads = lax.broadcasted_iota(jnp.int32, allowed_ref.shape, 1)
    def part_of(part, head):
        columns = slice(head * HD, (head + 1) * HD)
        return got_ref[:, part * rows : (part + 1) * rows, columns].reshape(-1, HD)

    scores = [
        lax.dot_general(
            part_of(0, head), part_of(1, head), (((1,), (1,)), ((), ())),
            preferred_element_type=jnp.float32,
        )
        for head in range(per_dev)
    ]
    allowed = [
        jnp.max(jnp.where(heads == first + head, allowed_ref[...], 0), axis=1, keepdims=True) > 0
        for head in range(per_dev)
    ]
    weights = []
    for head in range(per_dev):
        masked = jnp.where(allowed[head], scores[head], big_negative)
        top = jnp.max(masked, axis=1, keepdims=True)
        weights.append(jnp.where(allowed[head], jnp.exp((masked - top) * HD ** (-0.5)), 0.0))
    for head in range(per_dev):
        summed = jnp.dot(
            weights[head].astype(jnp.bfloat16), part_of(2, head), preferred_element_type=jnp.float32
        )
        total = jnp.sum(weights[head], axis=1, keepdims=True)
        out_ref[:, :, head * HD : (head + 1) * HD] = (
            (summed * (1.0 / total)).astype(jnp.bfloat16).reshape(sources, rows, HD)
        )


def one_tile(queries, keys, values, tile_mask):
    count = lax.axis_size(("head", "blk"))
    rows = queries.shape[0]
    per_dev = H // count
    width = per_dev * HD
    vmem = pl.BlockSpec(memory_space=pltpu.VMEM)
    packed = jnp.concatenate(
        [m.reshape(rows, count, width).transpose(1, 0, 2) for m in (queries, keys, values)],
        axis=1,
    )
    packed, tile_mask = lax.optimization_barrier((packed, tile_mask))
    allowed = (tile_mask.reshape(1, H) > 0).astype(jnp.int32)
    packed, allowed = lax.optimization_barrier((packed, allowed))
    exchange = functools.partial(
        lax.all_to_all,
        axis_name=("head", "blk"),
        split_axis=0,
        concat_axis=0,
        axis_index_groups=[slot_order()],
        tiled=True,
    )
    got = exchange(packed)
    result = pl.pallas_call(
        functools.partial(attend_kernel, per_dev=per_dev),
        out_shape=jax.ShapeDtypeStruct((count, rows, width), jnp.bfloat16),
        in_specs=[vmem] * 2,
        out_specs=vmem,
        compiler_params=pltpu.CompilerParams(vmem_limit_bytes=4 * 1024 * 1024),
    )(allowed, got)
    returned = exchange(result)
    return returned.transpose(1, 0, 2).reshape(rows, H * HD)


def on_device(queries, keys, values, tile_mask):
    count = lax.axis_size("head") * lax.axis_size("blk")
    same_rows = queries.shape[0] == keys.shape[0]
    if same_rows and queries.shape[0] * count == TILE and H % count == 0 and lax.axis_size("head") % 2 == 0:
        return one_tile(queries, keys, values, tile_mask)
    return general(queries, keys, values, tile_mask)


def solution(mesh):
    in_specs = (
        P(("groups", "head", "blk"), None),
        P(("groups", "head", "blk"), None),
        P(("groups", "head", "blk"), None),
        P("groups", None, None),
    )
    out_specs = P(("groups", "head", "blk"), None)
    return jax.shard_map(
        on_device, mesh=mesh, in_specs=in_specs, out_specs=out_specs, check_vma=False
    )
```
